256 devices in a mesh: grp: 4 (over y), shard: 64 (over z, x, core).
Axes of the slice: x: 4, y: 4, z: 8, core: 2. Of those that a mesh axis runs over, the one named last changes fastest.
Arguments:
- moe_input: bfloat16 [32768, 2048], P(('grp', 'shard')), may hold values from -6 to 6
- out_grad: bfloat16 [32768, 2048], P(('grp', 'shard')), may hold values from -6 to 6
- expert_ids: int32 [32768, 2], P(('grp', 'shard')), may hold values from 0 to 127, all different within a row; in each aligned block of 128 rows (0 to 127, 128 to 255, ...) at most 3 rows name the same one
- gate_weights: bfloat16 [32768, 2], P(('grp', 'shard')), may hold values from 0.099609375 to 1
- w_gate: bfloat16 [128, 768, 2048], P('shard', 'grp'), may hold values from -0.125 to 0.125
- w_up: bfloat16 [128, 768, 2048], P('shard', 'grp'), may hold values from -0.125 to 0.125
- w_down: bfloat16 [128, 768, 2048], P('shard', 'grp'), may hold values from -0.21875 to 0.21875
Outputs:
- input_grad: bfloat16 [32768, 2048], P(('grp', 'shard'))
- grad_gate: bfloat16 [128, 768, 2048], P('shard', 'grp')
- grad_up: bfloat16 [128, 768, 2048], P('shard', 'grp')
- grad_down: bfloat16 [128, 768, 2048], P('shard', 'grp')
The draws below stay inside these ranges and needn't reach their ends.
Inputs may be any that keep to these rules, and one draw needn't show every extreme that they name: `expert_ids`: each token names 2 different experts; within the 128 tokens of one device no expert is named more than 3 times, a bound that some block reaches.
All inputs are finite; a program needn't handle non-finite values.
Results may differ from the reference program's by a relative error of at most 0.0058.
Values may be sent and summed in bfloat16 or wider, within the bound.
No kernel may reach another device: no remote copies, remote signals or barrier semaphores. Data moves between devices by JAX's collectives and lax.ppermute only.
A program may use at most 192 MiB of HBM per device.

```python
import math
import jax
import jax.numpy as jnp
import numpy as np
from jax import lax

D = 2048
FF = 768
EXPERTS = 128
TOP = 2
TOK_DEV = 128
CAP = 3
TOKENS = 32768


def level_of(stream_key, extent, pieces, low, high):
    def one(dim, blocks):
        heights = jax.random.uniform(jax.random.fold_in(jax.random.fold_in(stream_key, 6), dim), (blocks,), jnp.float32, low / len(pieces), high / len(pieces))
        return jnp.repeat(jnp.exp(heights), extent[dim] // blocks).reshape((-1,) + (1,) * (len(extent) - dim - 1))

    gain = one(*pieces[0])
    for cut in pieces[1:]:
        gain = gain * one(*cut)
    return gain


def deal_out(own_key, own, number, rows, number_of, top, bound, lean):
    sequence = jax.random.permutation(own_key, number_of)
    packed, ordinary = shares(number_of, rows * top, bound, lean, True), shares(number_of, rows * top, bound, lean, False)
    places = jnp.arange(number_of)

    def named(sizes, rotation):
        used = int((sizes > 0).sum())
        fixed = max(1, used // 4)
        moved = fixed + (places - fixed + rotation * (used - fixed)) % max(1, number_of - fixed)
        return jnp.zeros((number_of,), jnp.int32).at[sequence[jnp.where(places < fixed, places, moved)]].set(jnp.asarray(sizes, jnp.int32))

    sizes = jnp.where(number % 4 == 0, named(packed, number // 4), named(ordinary, number - number // 4 - 1))
    mixed = jax.random.permutation(jax.random.fold_in(own, 3), number_of)
    source_of, receiver = mixed[0:number_of // 2 * 2:2], mixed[1:number_of // 2 * 2:2]
    slack = jnp.minimum(sizes[source_of] - 1, bound - sizes[receiver]) // 2
    slack = jnp.where((source_of == sequence[0]) | (receiver == sequence[0]) | (sizes[receiver] == 0), 0, jnp.maximum(slack, 0))
    moved = jax.random.randint(jax.random.fold_in(own, 4), (number_of // 2,), 0, 1 << 20) % (slack + 1)
    sizes = sizes.at[source_of].add(-moved).at[receiver].add(moved)
    items = jnp.searchsorted(jnp.cumsum(sizes), jnp.arange(rows * top), side="right").astype(jnp.int32)
    grid = items.reshape(top, rows).T
    grid = grid[jax.random.permutation(jax.random.fold_in(own, 1), rows)]
    rotation = jax.random.randint(jax.random.fold_in(own, 2), (rows, 1), 0, top)
    return jnp.take_along_axis(grid, (jnp.arange(top)[None, :] + rotation) % top, axis=1)


def shares(count, total, bound, skew, full):
    weights = [(1 << 20) // math.isqrt(rank ** skew) + 1 for rank in range(1, count + 1)]
    largest = bound if full else min(bound, max(-(-total // count), total * weights[0] // sum(weights)))
    least = 1 if total - largest >= count - 1 else 0
    counts, spare = [largest] + [least] * (count - 1), total - largest - least * (count - 1)
    while spare > 0:
        movable = [i for i in range(1, count) if counts[i] < largest] or [i for i in range(1, count) if counts[i] < bound]
        pool, budget = sum([weights[i] for i in movable]), spare
        for i in movable:
            addition = min(bound - counts[i], max(1, budget * weights[i] // pool), spare)
            counts[i] = counts[i] + addition
            spare = spare - addition
    return np.array(counts)


def centred(rng, dims, spread, reach, pieces=(), held_as=jnp.bfloat16):
    drawn = jax.random.normal(rng, dims, jnp.float32) * spread
    if len(pieces) > 0:
        drawn = level_of(rng, dims, pieces, -0.22, 0.18) * drawn
    return jnp.clip(drawn, min=-reach, max=reach).astype(held_as)


def setup_inputs(seed: int = 0) -> dict:
    arg_keys = jax.random.split(jax.random.key(seed), 8)
    moe_input = centred(arg_keys[0], (TOKENS, D), 1.0, 6.0, ((0, 256),))
    out_grad = centred(arg_keys[1], (TOKENS, D), 1.0, 6.0, ((0, 256),))
    expert_ids_keys = jax.random.split(jax.random.fold_in(arg_keys[2], 1), TOKENS // TOK_DEV)
    expert_ids_turns = jax.random.permutation(jax.random.fold_in(arg_keys[2], 3), TOKENS // TOK_DEV)
    expert_ids = jax.vmap(lambda own, number: deal_out(jax.random.fold_in(arg_keys[2], 2), own, number, TOK_DEV, EXPERTS, TOP, CAP, 1))(expert_ids_keys, expert_ids_turns).reshape((TOKENS, TOP))
    gate_weights = jnp.clip(0.099609375 + 0.9003906 * jax.random.uniform(arg_keys[3], (TOKENS, TOP), jnp.float32) ** level_of(arg_keys[3], (TOKENS, TOP), ((0, 256),), -0.2, 0.2), 0.099609375, 1.0).astype(jnp.bfloat16)
    w_gate = centred(arg_keys[4], (EXPERTS, FF, D), D ** -0.5, 0.125, ((0, 64), (1, 4)))
    w_up = centred(arg_keys[5], (EXPERTS, FF, D), D ** -0.5, 0.125, ((0, 64), (1, 4)))
    w_down = centred(arg_keys[6], (EXPERTS, FF, D), FF ** -0.5, 0.21875, ((0, 64), (1, 4)))
    return {"moe_input": moe_input, "out_grad": out_grad, "expert_ids": expert_ids, "gate_weights": gate_weights, "w_gate": w_gate, "w_up": w_up, "w_down": w_down}


def silu_parts(pre_act):
    sigmoid_val = jax.nn.sigmoid(pre_act)
    return pre_act * sigmoid_val, sigmoid_val * (1.0 + pre_act * (1.0 - sigmoid_val))


def reference(moe_input, out_grad, expert_ids, gate_weights, w_gate, w_up, w_down):
    contract = (((1,), (1,)), ((), ()))
    contract_rows = (((0,), (0,)), ((), ()))
    blocks = TOKENS // TOK_DEV
    flat_ids = expert_ids.reshape(blocks, TOK_DEV * TOP)
    matches = (flat_ids[:, :, None] == jnp.arange(EXPERTS, dtype=jnp.int32)[None, None, :]).astype(jnp.int32)
    rank_of = jnp.sum((jnp.cumsum(matches, axis=1) - matches) * matches, axis=2).astype(jnp.int32)
    block_of = jnp.broadcast_to(jnp.arange(blocks, dtype=jnp.int32)[:, None], flat_ids.shape)
    token_of = block_of * TOK_DEV + jnp.broadcast_to(jnp.arange(TOK_DEV * TOP, dtype=jnp.int32)[None, :] // TOP, flat_ids.shape)
    slot_table = jnp.zeros((EXPERTS, blocks, CAP), jnp.int32).at[flat_ids, block_of, rank_of].set(token_of + 1)
    gate_table = jnp.zeros((EXPERTS, blocks, CAP), jnp.float32).at[flat_ids, block_of, rank_of].set(
        gate_weights.reshape(blocks, TOK_DEV * TOP).astype(jnp.float32))

    def expert_step(running, expert_item):
        row_index, gate_vals, weight_gate, weight_up, weight_down = expert_item
        occupied = row_index > 0
        position = jnp.maximum(row_index - 1, 0).astype(jnp.int32)
        inputs = jnp.where(occupied[:, None], moe_input[position], jnp.zeros((), moe_input.dtype))
        grads_in = jnp.where(occupied[:, None], out_grad[position], jnp.zeros((), out_grad.dtype))
        gated = (gate_vals[:, None] * grads_in.astype(jnp.float32)).astype(jnp.bfloat16)
        pre_gate = lax.dot_general(inputs, weight_gate, contract, preferred_element_type=jnp.float32)
        pre_up = lax.dot_general(inputs, weight_up, contract, preferred_element_type=jnp.float32)
        act_val, act_slope = silu_parts(pre_gate)
        activation = (act_val * pre_up).astype(jnp.bfloat16)
        act_grad = lax.dot_general(gated, weight_down, contract, preferred_element_type=jnp.float32)
        gate_grad = (act_grad * pre_up * act_slope).astype(jnp.bfloat16)
        up_grad = (act_grad * act_val).astype(jnp.bfloat16)
        down_sum = lax.dot_general(activation, gated, contract_rows, preferred_element_type=jnp.float32)
        gate_sum = lax.dot_general(gate_grad, inputs, contract_rows, preferred_element_type=jnp.float32)
        up_sum = lax.dot_general(up_grad, inputs, contract_rows, preferred_element_type=jnp.float32)
        terms = jnp.dot(gate_grad, weight_gate, preferred_element_type=jnp.float32) + jnp.dot(up_grad, weight_up, preferred_element_type=jnp.float32)
        running = running.at[position].add(jnp.where(occupied[:, None], terms, jnp.zeros((), terms.dtype)))
        return running, (gate_sum.astype(jnp.bfloat16), up_sum.astype(jnp.bfloat16), down_sum.astype(jnp.bfloat16))

    moe_grad, grads = lax.scan(
        expert_step,
        jnp.zeros((TOKENS, D), jnp.float32),
        (slot_table.reshape(EXPERTS, blocks * CAP), gate_table.reshape(EXPERTS, blocks * CAP), w_gate, w_up, w_down))
    input_grad = (out_grad.astype(jnp.float32) + moe_grad).astype(jnp.bfloat16)
    return input_grad, grads[0], grads[1], grads[2]
```

```python
import functools

import jax
import jax.numpy as jnp
from jax import lax
from jax.experimental import pallas as pl
from jax.experimental.pallas import tpu as pltpu
from jax.sharding import PartitionSpec as P

CAP = 3
BF = jnp.bfloat16
F32 = jnp.float32


NT = (((1,), (1,)), ((), ()))
TN = (((0,), (0,)), ((), ()))


def dot(a, b, dims=(((1,), (0,)), ((), ()))):
    return lax.dot_general(a, b, dims, preferred_element_type=F32)


def iota(shape, dim):
    return lax.broadcasted_iota(jnp.int32, shape, dim)


def one(mask):
    return jnp.where(mask, 1.0, 0.0).astype(BF)


def pack_kernel(ids_ref, gate_ref, x_ref, g_ref, o_ref, *, slot, half):
    rows, tokens = o_ref.shape[0], x_ref.shape[0]
    row = iota((rows, tokens), 0)
    expert = row >> 2
    first = ids_ref[0:1, :] == expert
    second = ids_ref[1:2, :] == expert
    before = one(iota((tokens, tokens), 0) < iota((tokens, tokens), 1))
    rank_first = dot(one(first), before)
    in_first = jnp.sum(jnp.where(first, 1.0, 0.0), axis=1, keepdims=True)
    rank_second = dot(one(second), before) + in_first
    take_first = first & (rank_first == float(slot))
    take_second = second & (rank_second == float(slot))
    plain = jnp.where(take_first | take_second, 1.0, 0.0)
    gates = gate_ref[...].astype(F32)
    scaled = jnp.where(take_first, gates[0:1, :], 0.0) + jnp.where(take_second, gates[1:2, :], 0.0)
    part = row & 3
    lhs = jnp.concatenate(
        [jnp.where(part == p, plain if p < 2 else scaled, 0.0).astype(BF) for p in range(4)], axis=1
    )
    rhs = jnp.concatenate(
        [x_ref[:, :half], x_ref[:, half:], g_ref[:, :half], g_ref[:, half:]], axis=0
    )
    o_ref[...] = dot(lhs, rhs).astype(BF)


def unpack_kernel(r_ref, o_ref, *, shards, half):
    rows, cols = o_ref.shape[0], r_ref.shape[0]
    out_row = iota((rows, cols), 0)
    block, source = out_row // shards, out_row % shards
    col = iota((rows, cols), 1)
    base = 8 * source + 4 * (block % 2) + 2 * (block // 2)
    received = r_ref[...]
    for h in range(2):
        o_ref[:, h * half : (h + 1) * half] = dot(one(col == base + h), received).astype(BF)


def expert_kernel(
    own_ref, left_ref, right_ref, far_x_ref, far_g_ref, wg_ref, wu_ref, wd_ref,
    fw_ref, bw_ref, keep_ref, mine_ref, act_ref, gg_ref, ug_ref,
):
    rows = own_ref.shape[2]
    x = jnp.concatenate([own_ref[0, 0], left_ref[0, 0], right_ref[0, 0], far_x_ref[0]], axis=0)
    g = jnp.concatenate([own_ref[1, 0], left_ref[1, 0], right_ref[1, 0], far_g_ref[0]], axis=0)
    wg, wu, wd = wg_ref[0], wu_ref[0], wd_ref[0]
    pre_gate = dot(wg, x, NT)
    pre_up = dot(wu, x, NT)
    act_grad = dot(wd, g, NT)
    s = jax.nn.sigmoid(pre_gate)
    val = pre_gate * s
    slope = s * (1.0 + pre_gate * (1.0 - s))
    act_ref[0] = (val * pre_up).astype(BF)
    gate_grad = (act_grad * pre_up * slope).astype(BF)
    up_grad = (act_grad * val).astype(BF)
    gg_ref[0] = gate_grad
    ug_ref[0] = up_grad
    hidden = (dot(gate_grad, wg, TN) + dot(up_grad, wu, TN)).astype(BF)
    mine, left, right, far = (hidden[k * rows : (k + 1) * rows] for k in range(4))
    mine_ref[0] = mine

    @pl.when(pl.program_id(0) == 0)
    def _():
        fw_ref[0] = far
        bw_ref[0] = left
        keep_ref[0] = right

    @pl.when(pl.program_id(0) == 1)
    def _():
        fw_ref[0] = right
        bw_ref[0] = far
        keep_ref[0] = left


def back_kernel(mine_ref, fw_ref, bw_ref, tf_ref, tb_ref, o_ref):
    shards, width = tf_ref.shape
    rows, quarter = o_ref.shape
    sums = (
        mine_ref[0].astype(F32) + bw_ref[0].astype(F32) + tf_ref[...].astype(F32),
        mine_ref[1].astype(F32) + fw_ref[1].astype(F32) + tb_ref[...].astype(F32),
    )
    stacked = jnp.concatenate(
        [s.astype(BF)[:, q * quarter : (q + 1) * quarter] for s in sums for q in range(4)], axis=0
    )
    out_row = iota((rows, rows), 0)
    col = iota((rows, rows), 1)
    pick = one(col == (out_row % 8) * shards + out_row // 8)
    o_ref[...] = dot(pick, stacked).astype(BF)


def combine_kernel(ids_ref, base_ref, *refs, slots):
    ret_refs, o_ref = refs[:-1], refs[-1]
    rows, quarter = ret_refs[0].shape
    tokens = ids_ref.shape[0]
    col = iota((tokens, rows), 1)
    expert = col >> 2
    first = ids_ref[:, 0:1] == expert
    second = ids_ref[:, 1:2] == expert
    before = one(iota((tokens, tokens), 1) < iota((tokens, tokens), 0))
    rank_first = dot(before, one(first))
    in_first = jnp.sum(jnp.where(first, 1.0, 0.0), axis=0, keepdims=True)
    rank_second = dot(before, one(second)) + in_first
    takes = [
        (first & (rank_first == float(slot))) | (second & (rank_second == float(slot)))
        for slot in slots
    ]
    part = col & 3
    for q in range(4):
        cols = slice(q * quarter, (q + 1) * quarter)
        total = base_ref[:, cols].astype(F32)
        for take, ret_ref in zip(takes, ret_refs):
            total += dot(one(take & (part == q)), ret_ref[...])
        o_ref[:, cols] = total.astype(o_ref.dtype)


def weight_kernel(*refs):
    gate_out, up_out, down_out = refs[-3:]
    sums = [None, None, None]
    for k in range(CAP):
        own, left, right, far_x, far_g, act, gg, ug = refs[8 * k : 8 * k + 8]
        x = jnp.concatenate([own[0, 0], left[0, 0], right[0, 0], far_x[0]], axis=0)
        g = jnp.concatenate([own[1, 0], left[1, 0], right[1, 0], far_g[0]], axis=0)
        for n, (a, b) in enumerate(((gg, x), (ug, x), (act, g))):
            term = dot(a[0], b)
            sums[n] = term if sums[n] is None else sums[n] + term
    for ref, total in zip((gate_out, up_out, down_out), sums):
        ref[0] = total.astype(BF)


def call(kernel, out_shape, *args, name, **kw):
    return pl.pallas_call(kernel, out_shape=out_shape, name=name, **kw)(*args)


def sds(shape, dtype=BF):
    return jax.ShapeDtypeStruct(shape, dtype)


def body(moe_input, out_grad, expert_ids, gate_weights, w_gate, w_up, w_down):
    shards = lax.axis_size("shard")
    groups = lax.axis_size("grp")
    per_device, hidden, width = w_gate.shape
    tokens = moe_input.shape[0]
    half, quarter = width // 2, width // 4
    rows = 8 * shards
    ids_t = expert_ids.T
    gates_t = gate_weights.T
    fwd = [(k, (k + 1) % groups) for k in range(groups)]
    bwd = [(k, (k - 1) % groups) for k in range(groups)]

    def exchange(a):
        return lax.all_to_all(a, "shard", split_axis=0, concat_axis=0, tiled=True)

    def pack(slot):
        return call(
            functools.partial(pack_kernel, slot=slot, half=half),
            sds((rows, half)), ids_t, gates_t, moe_input, out_grad, name=f"pack{slot}",
        )

    def unpack(received):
        return call(
            functools.partial(unpack_kernel, shards=shards, half=half),
            sds((4 * shards, width)), received, name="unpack",
        )

    def gather(own):
        n = 2 * shards
        left = lax.ppermute(own, "grp", fwd)
        right = lax.ppermute(own, "grp", bwd)
        far_x = lax.ppermute(left[:n], "grp", fwd)
        far_g = lax.ppermute(right[n:], "grp", bwd)
        four = (2, 2, shards, width)
        return (
            own.reshape(four), left.reshape(four), right.reshape(four),
            far_x.reshape(four[1:]), far_g.reshape(four[1:]),
        )

    def experts(rows_in):
        pair = pl.BlockSpec((2, 1, shards, width), lambda e: (0, e, 0, 0))
        single = pl.BlockSpec((1, shards, width), lambda e: (e, 0, 0))
        weight = pl.BlockSpec((1, hidden, width), lambda e: (e, 0, 0))
        small = pl.BlockSpec((1, hidden, groups * shards), lambda e: (e, 0, 0))
        row_out, small_out = sds((2, shards, width)), sds((2, hidden, groups * shards))
        return call(
            expert_kernel, (row_out,) * 4 + (small_out,) * 3, *rows_in, w_gate, w_up, w_down,
            name="experts", grid=(per_device,),
            in_specs=[pair] * 3 + [single] * 2 + [weight] * 3,
            out_specs=[single] * 4 + [small] * 3,
        )

    def scatter(fw, bw, keep, mine):
        fw_in = lax.ppermute(fw, "grp", fwd)
        bw_in = lax.ppermute(bw, "grp", bwd)
        tf = (fw_in[0].astype(F32) + keep[0].astype(F32)).astype(BF)
        tb = (bw_in[1].astype(F32) + keep[1].astype(F32)).astype(BF)
        tf_in = lax.ppermute(tf, "grp", fwd)
        tb_in = lax.ppermute(tb, "grp", bwd)
        return call(
            back_kernel, sds((rows, quarter)), mine, fw_in, bw_in, tf_in, tb_in, name="back"
        )

    def combine(base, rets, slots, dtype):
        return call(
            functools.partial(combine_kernel, slots=slots),
            sds((tokens, width), dtype), expert_ids, base, *rets, name="combine",
        )

    gathered, small, returned = [], [], []
    sent = [exchange(pack(slot)) for slot in range(CAP)]
    for slot in range(CAP):
        gathered.append(gather(unpack(sent[slot])))
    for slot in range(CAP):
        fw, bw, keep, mine, act, gg, ug = experts(gathered[slot])
        small.append((act, gg, ug))
        returned.append(exchange(scatter(fw, bw, keep, mine)))

    cols = 512
    pair = pl.BlockSpec((2, 1, shards, cols), lambda e, c: (0, e, 0, c))
    single = pl.BlockSpec((1, shards, cols), lambda e, c: (e, 0, c))
    smalls = pl.BlockSpec((1, hidden, groups * shards), lambda e, c: (e, 0, 0))
    weight = pl.BlockSpec((1, hidden, cols), lambda e, c: (e, 0, c))
    grads = call(
        weight_kernel, (sds(w_gate.shape),) * 3,
        *[a for k in range(CAP) for a in (*gathered[k], *small[k])],
        name="weights", grid=(per_device, width // cols),
        in_specs=([pair] * 3 + [single] * 2 + [smalls] * 3) * CAP,
        out_specs=[weight] * 3,
    )
    partial_sum = combine(out_grad, returned[:2], (0, 1), F32)
    input_grad = combine(partial_sum, returned[2:], (2,), BF)
    return (input_grad, *grads)


def solution(mesh):
    rows = P(("grp", "shard"), None)
    weights = P("shard", "grp", None)
    return jax.shard_map(
        body,
        mesh=mesh,
        in_specs=(rows,) * 4 + (weights,) * 3,
        out_specs=(rows,) + (weights,) * 3,
        check_vma=False,
    )
```

```python
import functools

import jax
import jax.numpy as jnp
from jax import lax
from jax.experimental import pallas as pl
from jax.experimental.pallas import tpu as pltpu
from jax.sharding import PartitionSpec as P


CAP = 3
BF = jnp.bfloat16
F32 = jnp.float32


VMEM = pl.BlockSpec(memory_space=pltpu.VMEM)
NT = (((1,), (1,)), ((), ()))


def dot(a, b, dims=(((1,), (0,)), ((), ()))):
    return lax.dot_general(a, b, dims, preferred_element_type=F32)


def iota(shape, dim):
    return lax.broadcasted_iota(jnp.int32, shape, dim)


def one(mask):
    return jnp.where(mask, 1.0, 0.0).astype(BF)


def pack_kernel(ids_ref, gate_ref, x_ref, g_ref, o_ref, *, slot, half):
    rows, tokens = o_ref.shape[0], x_ref.shape[0]
    row = iota((rows, tokens), 0) + pl.program_id(0) * rows
    expert = row >> 2
    first = ids_ref[0:1, :] == expert
    second = ids_ref[1:2, :] == expert
    before = one(iota((tokens, tokens), 0) < iota((tokens, tokens), 1))
    rank_first = dot(one(first), before)
    in_first = jnp.sum(jnp.where(first, 1.0, 0.0), axis=1, keepdims=True)
    rank_second = dot(one(second), before) + in_first
    take_first = first & (rank_first == float(slot))
    take_second = second & (rank_second == float(slot))
    plain = jnp.where(take_first | take_second, 1.0, 0.0)
    gates = gate_ref[...].astype(F32)
    scaled = jnp.where(take_first, gates[0:1, :], 0.0) + jnp.where(take_second, gates[1:2, :], 0.0)
    part = row & 3
    lhs = jnp.concatenate(
        [jnp.where(part == p, plain if p < 2 else scaled, 0.0).astype(BF) for p in range(4)], axis=1
    )
    rhs = jnp.concatenate(
        [x_ref[:, :half], x_ref[:, half:], g_ref[:, :half], g_ref[:, half:]], axis=0
    )
    o_ref[...] = dot(lhs, rhs).astype(BF)


def unpack_kernel(r_ref, o_ref, *, shards, half):
    rows = r_ref.shape[0] // 2
    near = rows // 8
    row, col = iota((rows, rows), 0), iota((rows, rows), 1)
    pick = one(col == row % near * 8 + row // near)
    for block in range(2):
        got = dot(pick, r_ref[block * rows : (block + 1) * rows]).astype(BF)
        for part in range(8):
            expert, array, side = part // 4, part // 2 % 2, part % 2
            start = (2 * array + expert) * shards + block * near
            o_ref[start : start + near, side * half : (side + 1) * half] = got[
                part * near : (part + 1) * near
            ]


def expert_kernel(
    own_ref, left_ref, right_ref, far_x_ref, far_g_ref, wg_ref, wu_ref, wd_ref,
    fw_ref, bw_ref, keep_ref, mine_ref, act_ref, gg_ref, ug_ref, pre_ref, turned_ref, *, block,
):
    rows, width = own_ref.shape[2:]
    hidden = wg_ref.shape[1]
    pre_ref[...] = jnp.zeros_like(pre_ref)

    def part(k):
        return pl.ds(pl.multiple_of(k * block, block), block)

    def both(cols):
        return jnp.concatenate([wg_ref[0, :, cols], wu_ref[0, :, cols]], axis=0)

    def forward(k, _):
        cols = part(k)
        near = (own_ref, left_ref, right_ref)
        x = jnp.concatenate([r[0, 0, :, cols] for r in near] + [far_x_ref[0, :, cols]], axis=0)
        g = jnp.concatenate([r[1, 0, :, cols] for r in near] + [far_g_ref[0, :, cols]], axis=0)
        pre_ref[: 2 * hidden] += dot(both(cols), x, NT)
        pre_ref[2 * hidden :] += dot(wd_ref[0, :, cols], g, NT)
        return 0

    lax.fori_loop(0, width // block, forward, 0)
    pre_gate, pre_up = pre_ref[:hidden], pre_ref[hidden : 2 * hidden]
    act_grad = pre_ref[2 * hidden :]
    s = jax.nn.sigmoid(pre_gate)
    val = pre_gate * s
    slope = s * (1.0 + pre_gate * (1.0 - s))
    act_ref[0] = (val * pre_up).astype(BF)
    gate_grad = (act_grad * pre_up * slope).astype(BF)
    up_grad = (act_grad * val).astype(BF)
    gg_ref[0] = gate_grad
    ug_ref[0] = up_grad
    turned_ref[...] = jnp.concatenate([gate_grad, up_grad], axis=0).T
    even = pl.program_id(0) == 0

    def backward(k, _):
        cols = part(k)
        sums = dot(turned_ref[...], both(cols)).astype(BF)
        mine, left, right, far = (sums[n * rows : (n + 1) * rows] for n in range(4))
        mine_ref[0, :, cols] = mine
        fw_ref[0, :, cols] = jnp.where(even, far, right)
        bw_ref[0, :, cols] = jnp.where(even, left, far)
        keep_ref[0, :, cols] = jnp.where(even, right, left)
        return 0

    lax.fori_loop(0, width // block, backward, 0)


def relay_kernel(fw_ref, bw_ref, keep_ref, tf_ref, tb_ref):
    tf_ref[...] = (fw_ref[0].astype(F32) + keep_ref[0].astype(F32)).astype(BF)
    tb_ref[...] = (bw_ref[1].astype(F32) + keep_ref[1].astype(F32)).astype(BF)


def back_kernel(mine_ref, fw_ref, bw_ref, tf_ref, tb_ref, o_ref):
    shards = tf_ref.shape[0]
    rows, quarter = o_ref.shape[0] // 2, o_ref.shape[1]
    near = shards // 2
    row, col = iota((rows, rows), 0), iota((rows, rows), 1)
    pick = one(col == row % 8 * near + row // 8)
    sums = (
        mine_ref[0].astype(F32) + bw_ref[0].astype(F32) + tf_ref[...].astype(F32),
        mine_ref[1].astype(F32) + fw_ref[1].astype(F32) + tb_ref[...].astype(F32),
    )
    sums = [s.astype(BF) for s in sums]
    for block in range(2):
        stacked = jnp.concatenate(
            [
                s[block * near : (block + 1) * near, q * quarter : (q + 1) * quarter]
                for s in sums
                for q in range(4)
            ],
            axis=0,
        )
        o_ref[block * rows : (block + 1) * rows] = dot(pick, stacked).astype(BF)


def combine_kernel(ids_ref, base_ref, ret_ref, o_ref, take_ref, *, slot):
    rows, quarter = ret_ref.shape
    tokens = ids_ref.shape[0]
    col = iota((tokens, rows), 1)
    expert = col >> 2
    first = ids_ref[:, 0:1] == expert
    second = ids_ref[:, 1:2] == expert
    before = one(iota((tokens, tokens), 1) < iota((tokens, tokens), 0))
    rank_first = dot(before, one(first))
    in_first = jnp.sum(jnp.where(first, 1.0, 0.0), axis=0, keepdims=True)
    rank_second = dot(before, one(second)) + in_first
    take = (first & (rank_first == float(slot))) | (second & (rank_second == float(slot)))
    take_ref[...] = jnp.where(take, (col & 3).astype(F32), -1.0)

    def add(q, _):
        cols = pl.ds(pl.multiple_of(q * quarter, quarter), quarter)
        term = dot(one(take_ref[...] == q.astype(F32)), ret_ref[...])
        o_ref[:, cols] = (base_ref[:, cols].astype(F32) + term).astype(o_ref.dtype)
        return 0

    lax.fori_loop(0, 4, add, 0)


def weight_kernel(*refs):
    gate_out, up_out, down_out = refs[-3:]
    sums = [None, None, None]
    for k in range(CAP):
        own, left, right, far_x, far_g, act, gg, ug = refs[8 * k : 8 * k + 8]
        x = jnp.concatenate([own[0, 0], left[0, 0], right[0, 0], far_x[0]], axis=0)
        g = jnp.concatenate([own[1, 0], left[1, 0], right[1, 0], far_g[0]], axis=0)
        for n, (a, b) in enumerate(((gg, x), (ug, x), (act, g))):
            term = dot(a[0], b)
            sums[n] = term if sums[n] is None else sums[n] + term
    for ref, total in zip((gate_out, up_out, down_out), sums):
        ref[0] = total.astype(BF)


def call(kernel, out_shape, *args, **kw):
    return pl.pallas_call(kernel, out_shape=out_shape, **kw)(*args)


def place(*arrays):
    placed = tuple(pltpu.with_memory_space_constraint(a, pltpu.VMEM) for a in arrays)
    return placed if len(placed) > 1 else placed[0]


def sds(shape, dtype=BF):
    return jax.ShapeDtypeStruct(shape, dtype)


def step(moe_input, out_grad, expert_ids, gate_weights, w_gate, w_up, w_down):
    shards = lax.axis_size("shard")
    groups = lax.axis_size("grp")
    per_device, hidden, width = w_gate.shape
    tokens = moe_input.shape[0]
    half, quarter = width // 2, width // 4
    rows = 8 * shards
    ids_t = expert_ids.T
    gates_t = gate_weights.T
    fwd = [(k, (k + 1) % groups) for k in range(groups)]
    bwd = [(k, (k - 1) % groups) for k in range(groups)]

    def fixed(shape):
        return pl.BlockSpec(shape, lambda r: (0,) * len(shape))

    def exchange(a):
        return lax.all_to_all(a, "shard", split_axis=0, concat_axis=0, tiled=True)

    def shift(a, pairs):
        return lax.ppermute(a, "grp", pairs)

    def pack(c):
        args = (ids_t, gates_t, moe_input, out_grad)
        return call(
            functools.partial(pack_kernel, slot=c, half=half),
            sds((rows, half)), *args, grid=(2,),
            in_specs=[fixed(a.shape) for a in args],
            out_specs=pl.BlockSpec((rows // 2, half), lambda r: (r, 0)),
        )

    def unpack(received):
        return call(
            functools.partial(unpack_kernel, shards=shards, half=half),
            sds((4 * shards, width)), place(received),
            in_specs=[VMEM], out_specs=VMEM,
        )

    def gather(own):
        n = 2 * shards
        left, right = shift(own, fwd), shift(own, bwd)
        far_x, far_g = shift(left[:n], fwd), shift(right[n:], bwd)
        four = (2, 2, shards, width)
        return (
            own.reshape(four), left.reshape(four), right.reshape(four),
            far_x.reshape(four[1:]), far_g.reshape(four[1:]),
        )

    def experts(rows_in):
        pair = pl.BlockSpec((2, 1, shards, width), lambda e: (0, e, 0, 0))
        single = pl.BlockSpec((1, shards, width), lambda e: (e, 0, 0))
        weight = pl.BlockSpec((1, hidden, width), lambda e: (e, 0, 0))
        small = pl.BlockSpec((1, hidden, groups * shards), lambda e: (e, 0, 0))
        row_out, small_out = sds((2, shards, width)), sds((2, hidden, groups * shards))
        return call(
            functools.partial(expert_kernel, block=512),
            (row_out,) * 4 + (small_out,) * 3, *rows_in, w_gate, w_up, w_down,
            grid=(per_device,),
            in_specs=[pair] * 3 + [single] * 2 + [weight] * 3,
            out_specs=[single] * 4 + [small] * 3,
            scratch_shapes=[
                pltpu.VMEM((3 * hidden, groups * shards), F32),
                pltpu.VMEM((groups * shards, 2 * hidden), BF),
            ],
        )

    def scatter(fw, bw, keep, mine):
        fw_in, bw_in = shift(fw, fwd), shift(bw, bwd)
        tf, tb = call(
            relay_kernel, (sds((shards, width)),) * 2, *place(fw_in, bw_in), keep,
            in_specs=[VMEM] * 3, out_specs=[VMEM] * 2,
        )
        tf_in, tb_in = shift(tf, fwd), shift(tb, bwd)
        return call(
            back_kernel, sds((rows, quarter)), mine, *place(fw_in, bw_in, tf_in, tb_in),
            in_specs=[VMEM] * 5, out_specs=VMEM,
        )

    def combine(base, returned, slot, dtype):
        return call(
            functools.partial(combine_kernel, slot=slot),
            sds((tokens, width), dtype), expert_ids, base, place(returned),
            in_specs=[VMEM] * 3, out_specs=VMEM,
            scratch_shapes=[pltpu.VMEM((tokens, rows), F32)],
        )

    gathered, small, returned = [], [], []
    for c in range(CAP):
        gathered.append(gather(unpack(exchange(pack(c)))))
    for c in range(CAP):
        fw, bw, keep, mine, act, gg, ug = experts(gathered[c])
        small.append((act, gg, ug))
        returned.append(exchange(scatter(fw, bw, keep, mine)))

    cols = 512
    pair = pl.BlockSpec((2, 1, shards, cols), lambda e, c: (0, e, 0, c))
    single = pl.BlockSpec((1, shards, cols), lambda e, c: (e, 0, c))
    smalls = pl.BlockSpec((1, hidden, groups * shards), lambda e, c: (e, 0, 0))
    weight = pl.BlockSpec((1, hidden, cols), lambda e, c: (e, 0, c))
    grads = call(
        weight_kernel, (sds(w_gate.shape),) * 3,
        *[a for k in range(CAP) for a in (*gathered[k], *small[k])],
        grid=(per_device, width // cols),
        in_specs=([pair] * 3 + [single] * 2 + [smalls] * 3) * CAP,
        out_specs=[weight] * 3,
    )
    total = out_grad
    for c in range(CAP):
        total = combine(total, returned[c], c, F32 if c + 1 < CAP else BF)
    return (total, *grads)


def solution(mesh):
    rows = P(("grp", "shard"), None)
    weights = P("shard", "grp", None)
    return jax.shard_map(
        step,
        mesh=mesh,
        in_specs=(rows,) * 4 + (weights,) * 3,
        out_specs=(rows,) + (weights,) * 3,
        check_vma=False,
    )
```
